1024 devices in a mesh: row: 16 (over x, z_lo), col: 64 (over y, z_hi, core).
Axes of the slice: x: 8, y: 8, z: 8 (z_hi: 4, z_lo: 2; z = z_hi * 2 + z_lo), core: 2. Of those that a mesh axis runs over, the one named last changes fastest.
Arguments:
- tokens: bfloat16 [256, 10240], P('col', 'row'), may hold values from -6 to 6
- out_grad: bfloat16 [256, 10240], P('col', 'row'), may hold values from -3 to 3
- gate_weight: bfloat16 [10240, 26624], P('row', 'col'), may hold values from -0.0625 to 0.0625
- up_weight: bfloat16 [10240, 26624], P('row', 'col'), may hold values from -0.0625 to 0.0625
- down_weight: bfloat16 [26624, 10240], P('col', 'row'), may hold values from -0.0390625 to 0.0390625
- gate_mask: int32 [2560, 6656], P('row', 'col'), may hold values from 0 to 23
- up_mask: int32 [2560, 6656], P('row', 'col'), may hold values from 0 to 23
- down_mask: int32 [6656, 2560], P('col', 'row'), may hold values from 0 to 23
Outputs:
- input_grad: bfloat16 [256, 10240], P('col', 'row')
- gate_weight_grad: bfloat16 [10240, 26624], P('row', 'col')
- up_weight_grad: bfloat16 [10240, 26624], P('row', 'col')
- down_weight_grad: bfloat16 [26624, 10240], P('col', 'row')
The draws below stay inside these ranges and needn't reach their ends.
Inputs may be any that keep to these rules, and one draw needn't show every extreme that they name: `gate_mask`: each entry is a pattern code as the first step defines, so every row and every column of each 4 by 4 block of a pruned weight keeps exactly two entries. `up_mask`: as for gate_mask. `down_mask`: as for gate_mask.
All inputs are finite; a program needn't handle non-finite values.
Results may differ from the reference program's by a relative error of at most 0.0049.
Values may be sent and summed in bfloat16 or wider, within the bound.
A program may use at most 32 MiB of HBM per device.

```python
import jax
import jax.numpy as jnp
from jax import lax

D = 10240
FF = 26624
TOKENS = 256


def set_ends(drawn, own_key, low, top_value):
    longest = drawn.shape.index(max(drawn.shape))
    spots = []
    for shift in (0, 1):
        where = [jax.random.randint(jax.random.fold_in(own_key, axis), (), 0, length) for axis, length in enumerate(drawn.shape)]
        where[longest] = (where[longest] + shift) % drawn.shape[longest]
        spots.append(tuple(where))
    return drawn.at[spots[0]].set(low).at[spots[1]].set(top_value)


def block_levels(rng, shape, split, smallest, high):
    level = 1.0
    for axis_at, blocks in split:
        heights = jax.random.uniform(jax.random.fold_in(jax.random.fold_in(rng, 6), axis_at), (blocks,), jnp.float32, smallest / len(split), high / len(split))
        level = level * jnp.repeat(jnp.exp(heights), shape[axis_at] // blocks).reshape((-1,) + (1,) * (len(shape) - 1 - axis_at))
    return level


def normal_values(stream_key, dims, scale, reach, split=(), kind=jnp.bfloat16):
    drawn = scale * jax.random.normal(stream_key, dims, jnp.float32)
    if split:
        drawn = drawn * block_levels(stream_key, dims, split, -0.22, 0.18)
    return jnp.clip(drawn, -reach, reach).astype(kind)


def setup_inputs(seed: int = 0) -> dict:
    splits = jax.random.split(jax.random.key(seed), 9)
    return {
        "tokens": normal_values(splits[0], (TOKENS, D), 1.0, 6.0, ((0, 64), (1, 16))),
        "out_grad": normal_values(splits[1], (TOKENS, D), 0.5, 3.0, ((0, 64), (1, 16))),
        "gate_weight": normal_values(splits[2], (D, FF), D ** -0.5, 0.0625, ((0, 16), (1, 64))),
        "up_weight": normal_values(splits[3], (D, FF), D ** -0.5, 0.0625, ((0, 16), (1, 64))),
        "down_weight": normal_values(splits[4], (FF, D), FF ** -0.5, 0.0390625, ((0, 64), (1, 16))),
        "gate_mask": set_ends(jax.random.randint(splits[5], (D // 4, FF // 4), 0, 24), jax.random.fold_in(splits[5], 1), 0, 23).astype(jnp.int32),
        "up_mask": set_ends(jax.random.randint(splits[6], (D // 4, FF // 4), 0, 24), jax.random.fold_in(splits[6], 1), 0, 23).astype(jnp.int32),
        "down_mask": set_ends(jax.random.randint(splits[7], (FF // 4, D // 4), 0, 24), jax.random.fold_in(splits[7], 1), 0, 23).astype(jnp.int32),
    }


def expand_mask(block_ids):
    lead_col = block_ids // 6
    second_rank = (block_ids // 2) % 3
    third_rank = block_ids % 2
    second_col = second_rank + (second_rank >= lead_col).astype(jnp.int32)
    low_col = jnp.minimum(lead_col, second_col)
    high_col = jnp.maximum(lead_col, second_col)
    rest_low = jnp.where(low_col > 0, 0, jnp.where(high_col > 1, 1, 2)).astype(jnp.int32)
    rest_high = 6 - low_col - high_col - rest_low
    third_col = jnp.where(third_rank == 0, rest_low, rest_high)
    fourth_col = 6 - lead_col - second_col - third_col
    ordering = jnp.stack([lead_col, second_col, third_col, fourth_col], axis=-1)
    next_cols = jnp.roll(ordering, -1, axis=-1)
    column_ids = jnp.arange(4, dtype=jnp.int32)
    chosen = (ordering[..., :, None] == column_ids) | (next_cols[..., :, None] == column_ids)
    group_rows, group_cols = block_ids.shape
    pattern = chosen.transpose(0, 2, 1, 3).reshape(4 * group_rows, 4 * group_cols)
    return pattern.astype(jnp.bfloat16)


def swiglu_back(gate_sum, up_sum, back_sum):
    logistic = jax.nn.sigmoid(gate_sum)
    swish_val = gate_sum * logistic
    hidden = (swish_val * up_sum).astype(jnp.bfloat16)
    up_grad = (back_sum * swish_val).astype(jnp.bfloat16)
    gate_grad = (back_sum * up_sum * logistic * (1.0 + gate_sum * (1.0 - logistic))).astype(jnp.bfloat16)
    return gate_grad, up_grad, hidden


def reference(tokens, out_grad, gate_weight, up_weight, down_weight, gate_mask, up_mask, down_mask):
    block_width = 2048 if FF % 2048 == 0 else FF
    block_count = FF // block_width
    gate_blocks = gate_weight.reshape(D, block_count, block_width).transpose(1, 0, 2)
    up_blocks = up_weight.reshape(D, block_count, block_width).transpose(1, 0, 2)
    down_blocks = down_weight.reshape(block_count, block_width, D)
    gate_codes = gate_mask.reshape(D // 4, block_count, block_width // 4).transpose(1, 0, 2)
    up_codes = up_mask.reshape(D // 4, block_count, block_width // 4).transpose(1, 0, 2)
    down_codes = down_mask.reshape(block_count, block_width // 4, D // 4)

    def one_block(input_acc, pieces):
        gate_w, up_w, down_w, gate_c, up_c, down_c = pieces
        gate_keep = expand_mask(gate_c)
        up_keep = expand_mask(up_c)
        down_keep = expand_mask(down_c)
        gate_pruned = gate_w * gate_keep
        up_pruned = up_w * up_keep
        down_pruned = down_w * down_keep
        gate_sum = jnp.dot(tokens, gate_pruned, preferred_element_type=jnp.float32)
        up_sum = jnp.dot(tokens, up_pruned, preferred_element_type=jnp.float32)
        back_sum = jnp.dot(out_grad, down_pruned.T, preferred_element_type=jnp.float32)
        gate_grad, up_grad, hidden = swiglu_back(gate_sum, up_sum, back_sum)
        input_acc = input_acc + jnp.dot(gate_grad, gate_pruned.T, preferred_element_type=jnp.float32)
        input_acc = input_acc + jnp.dot(up_grad, up_pruned.T, preferred_element_type=jnp.float32)
        gate_wg = (jnp.dot(tokens.T, gate_grad, preferred_element_type=jnp.float32) * gate_keep).astype(jnp.bfloat16)
        up_wg = (jnp.dot(tokens.T, up_grad, preferred_element_type=jnp.float32) * up_keep).astype(jnp.bfloat16)
        down_wg = (jnp.dot(hidden.T, out_grad, preferred_element_type=jnp.float32) * down_keep).astype(jnp.bfloat16)
        return input_acc, (gate_wg, up_wg, down_wg)

    start_acc = jnp.zeros((TOKENS, D), jnp.float32)
    input_acc, outputs = lax.scan(one_block, start_acc, (gate_blocks, up_blocks, down_blocks, gate_codes, up_codes, down_codes))
    gate_wg, up_wg, down_wg = outputs
    gate_weight_grad = gate_wg.transpose(1, 0, 2).reshape(D, FF)
    up_weight_grad = up_wg.transpose(1, 0, 2).reshape(D, FF)
    down_weight_grad = down_wg.reshape(FF, D)
    return input_acc.astype(jnp.bfloat16), gate_weight_grad, up_weight_grad, down_weight_grad
```

```python
import functools

import jax
import jax.numpy as jnp
from jax import lax
from jax.experimental import pallas as pl
from jax.experimental.pallas import tpu as pltpu
from jax.sharding import PartitionSpec as P

F32 = jnp.float32
BF16 = jnp.bfloat16
MESH = pl.DeviceIdType.MESH
TILE = 16


def dot(left, right, at):
    return lax.dot_general(
        left, right, (((at[0],), (at[1],)), ((), ())), preferred_element_type=F32
    )


def orderings(code):
    def step(value, bound):
        return (value >= bound).astype(jnp.int32)

    p0 = step(code, 6) + step(code, 12) + step(code, 18)
    rest = code - 6 * p0
    rank1 = step(rest, 2) + step(rest, 4)
    rank2 = rest - 2 * rank1
    p1 = rank1 + (rank1 >= p0).astype(jnp.int32)
    low, high = jnp.minimum(p0, p1), jnp.maximum(p0, p1)
    rest_low = jnp.where(low > 0, 0, jnp.where(high > 1, 1, 2))
    rest_high = 6 - low - high - rest_low
    p2 = jnp.where(rank2 == 0, rest_low, rest_high)
    return p0, p1, p2, 6 - p0 - p1 - p2


def nibbles(code, bits_are_columns):
    p = orderings(code)
    one = jnp.ones_like(code)
    kept = []
    for at in range(4):
        if bits_are_columns:
            kept.append((one << p[at]) | (one << p[(at + 1) % 4]))
        else:
            bits = jnp.zeros_like(code)
            for i in range(4):
                hit = (p[i] == at) | (p[(i + 1) % 4] == at)
                bits = bits | jnp.where(hit, 1 << i, 0)
            kept.append(bits)
    return [k.astype(F32).astype(BF16) for k in kept]


def expanded(code, bits_are_columns, width, height):
    quarter = width // 4
    parts = nibbles(code, bits_are_columns)
    wide = jnp.zeros((code.shape[1], width), F32)
    d = lax.broadcasted_iota(jnp.int32, (quarter, width), 1)
    a = lax.broadcasted_iota(jnp.int32, (quarter, width), 0)
    for i in range(4):
        spread = (d == 4 * a + i).astype(F32).astype(BF16)
        wide = wide + dot(parts[i], spread, (0, 0))
    f = lax.broadcasted_iota(jnp.int32, (height, height // 4), 0)
    b = lax.broadcasted_iota(jnp.int32, (height, height // 4), 1)
    tall = dot(((f >> 2) == b).astype(F32).astype(BF16), wide.astype(BF16), (1, 0))
    local = lax.broadcasted_iota(jnp.int32, (height, width), 0) & 3
    return ((tall.astype(jnp.int32) >> local) & 1).astype(F32)


def kernel(
    dims,
    tok, og, gw, uw, dw, gm, um, dm,
    ig, gwg, uwg, dwg,
    zin, allt, allo, wcat, wdown, keep,
    zl_gu_out, zl_gu_in, zl_b_out, zl_b_in, sum_gu, sum_b,
    x_gu_out, x_gu_in, x_b_out, x_b_in, gu, hid,
    core_out, core_in, own, y_out, y_in, z_out, z_in,
    az_s, az_r, ay_s, ay_r, ac_s, ac_r,
    bz_s, bz_r, bx_s, bx_r,
    cx_s, cx_r, cz_s, cz_r,
    dc_s, dc_r, dy_s, dy_r, dz_s, dz_r,
):
    nx, nl, ny, nz, nc = dims
    row, col = lax.axis_index("row"), lax.axis_index("col")
    x, zl = row // nl, row % nl
    core = col % nc
    z = (col // nc) % nz
    y = col // (nc * nz)
    height, width = dw.shape
    rows = tok.shape[0]
    half = ny * TILE

    def x_peer(by):
        return (lax.rem(x + by, nx) * nl + zl, col)

    def y_peer(by):
        return (row, (lax.rem(y + by, ny) * nz + z) * nc + core)

    def z_peer(by):
        return (row, (y * nz + lax.rem(z + by, nz)) * nc + core)

    zl_peer = (x * nl + (1 - zl), col)
    core_peer = (row, (y * nz + z) * nc + (1 - core))

    peers = [x_peer(by) for by in range(1, nx)] + [y_peer(by) for by in range(1, ny)]
    peers += [z_peer(by) for by in range(1, nz)] + [zl_peer, core_peer]
    barrier = pltpu.get_barrier_semaphore()
    for peer in peers:
        pl.semaphore_signal(barrier, inc=1, device_id=peer, device_id_type=MESH)

    started = []

    def send(src, dst, s, r, peer):
        copy = pltpu.make_async_remote_copy(
            src_ref=src, dst_ref=dst, send_sem=s, recv_sem=r,
            device_id=peer, device_id_type=MESH,
        )
        copy.start()
        started.append(copy)
        return copy

    def block(at):
        return pl.ds(pl.multiple_of(at * TILE, TILE), TILE)

    def part(at):
        return pl.ds(pl.multiple_of(at * half, half), half)

    def order(n):
        return sorted(range(1, n), key=lambda by: min(by, n - by))

    gate_keep = expanded(gm[...], True, width, height)
    keep[pl.ds(0, height), :] = gate_keep.astype(BF16)
    wcat[pl.ds(0, height), :] = (gw[...].astype(F32) * gate_keep).astype(BF16)

    pl.semaphore_wait(barrier, len(peers))

    az = [
        [send(ref, zin.at[k, z], az_s.at[k, by], az_r.at[k, by], z_peer(by)) for by in range(1, nz)]
        for k, ref in enumerate((tok, og))
    ]

    up_keep = expanded(um[...], True, width, height)
    keep[pl.ds(height, height), :] = up_keep.astype(BF16)
    wcat[pl.ds(height, height), :] = (uw[...].astype(F32) * up_keep).astype(BF16)

    ay, ac = [], []
    for k, (ref, full) in enumerate(((tok, allt), (og, allo))):
        zin[k, z] = ref[...]
        for copy in az[k]:
            copy.wait_recv()
        gathered = jnp.concatenate([zin[k, i].astype(F32) for i in range(nz)], axis=0)
        here = block(core * ny + y)
        full[here, :] = gathered.astype(BF16)
        ay.append(
            {
                by: send(full.at[here, :], full.at[here, :], ay_s.at[k, by], ay_r.at[k, by], y_peer(by))
                for by in order(ny)
            }
        )
        ac.append([send(full.at[here, :], full.at[here, :], ac_s.at[k, 0], ac_r.at[k, 0], core_peer)])

    down_keep = expanded(dm[...], False, width, height)
    keep[pl.ds(2 * height, height), :] = down_keep.astype(BF16)
    wdown[...] = (dw[...].astype(F32) * down_keep).astype(BF16)

    def finish_gather(k, full):
        for by in order(ny):
            ay[k][by].wait_recv()
            there = block(core * ny + lax.rem(y + ny - by, ny))
            ac[k].append(
                send(full.at[there, :], full.at[there, :], ac_s.at[k, by], ac_r.at[k, by], core_peer)
            )
        for copy in ac[k]:
            copy.wait_recv()

    finish_gather(0, allt)
    zl_gu_out[...] = dot(allt[part(1 - zl), :], wcat[...], (1, 1)).astype(BF16)
    bz_gu = send(zl_gu_out, zl_gu_in, bz_s.at[0], bz_r.at[0], zl_peer)
    sum_gu[...] = dot(allt[part(zl), :], wcat[...], (1, 1))
    finish_gather(1, allo)
    zl_b_out[...] = dot(allo[part(1 - zl), :], wdown[...], (1, 1)).astype(BF16)
    bz_b = send(zl_b_out, zl_b_in, bz_s.at[1], bz_r.at[1], zl_peer)
    sum_b[...] = dot(allo[part(zl), :], wdown[...], (1, 1))

    bx = []
    for k, (first, arrived, total, out, into) in enumerate(
        ((bz_gu, zl_gu_in, sum_gu, x_gu_out, x_gu_in), (bz_b, zl_b_in, sum_b, x_b_out, x_b_in))
    ):
        first.wait_recv()
        paired = total[...] + arrived[...].astype(F32)
        total[...] = paired
        out[...] = paired.astype(BF16)
        bx.append(
            [
                send(out.at[block(lax.rem(x + by, nx)), :], into.at[by], bx_s.at[k, by], bx_r.at[k, by], x_peer(by))
                for by in order(nx)
            ]
        )

    sums = []
    for k, (total, into) in enumerate(((sum_gu, x_gu_in), (sum_b, x_b_in))):
        value = total[block(x), :]
        for copy, by in zip(bx[k], order(nx)):
            copy.wait_recv()
            value = value + into[by].astype(F32)
        sums.append(value)

    gate, up, back = sums[0][:, :height], sums[0][:, height:], sums[1]
    logistic = 1.0 / (1.0 + jnp.exp(-gate))
    swish = gate * logistic
    up_grad = back * swish
    gate_grad = back * up * logistic * (1.0 + gate * (1.0 - logistic))
    mine = block(zl * nx + x)
    gu[mine, :] = jnp.concatenate([gate_grad, up_grad], axis=1).astype(BF16)
    hid[mine, :] = (swish * up).astype(BF16)

    cx, cz = [], []
    for k, full in enumerate((gu, hid)):
        cx.append(
            {
                by: send(full.at[mine, :], full.at[mine, :], cx_s.at[k, by], cx_r.at[k, by], x_peer(by))
                for by in order(nx)
            }
        )
        cz.append([send(full.at[mine, :], full.at[mine, :], cz_s.at[k, 0], cz_r.at[k, 0], zl_peer)])
    for k, full in enumerate((gu, hid)):
        for by in order(nx):
            cx[k][by].wait_recv()
            there = block(zl * nx + lax.rem(x + nx - by, nx))
            cz[k].append(
                send(full.at[there, :], full.at[there, :], cz_s.at[k, by], cz_r.at[k, by], zl_peer)
            )
        if k == 0:
            for copy in cz[k]:
                copy.wait_recv()
            core_out[...] = dot(gu[part(1 - core), :], wcat[...], (1, 0))
            dc = send(core_out, core_in, dc_s, dc_r, core_peer)
            own[...] = dot(gu[part(core), :], wcat[...], (1, 0))

    dc.wait_recv()
    total = own[...] + core_in[...]
    own[...] = total
    y_out[...] = total.astype(BF16)
    dy = [
        send(y_out.at[block(lax.rem(y + by, ny)), :], y_in.at[by], dy_s.at[by], dy_r.at[by], y_peer(by))
        for by in order(ny)
    ]

    gwg[...] = (dot(gu[:, :height], allt[...], (0, 0)) * keep[pl.ds(0, height), :].astype(F32)).astype(BF16)
    uwg[...] = (dot(gu[:, height:], allt[...], (0, 0)) * keep[pl.ds(height, height), :].astype(F32)).astype(BF16)

    value = own[block(y), :]
    for copy, by in zip(dy, order(ny)):
        copy.wait_recv()
        value = value + y_in[by].astype(F32)
    for i in range(nz):
        z_out[i] = value[i * rows : (i + 1) * rows, :]
    dz = [
        send(z_out.at[lax.rem(z + by, nz)], z_in.at[by], dz_s.at[by], dz_r.at[by], z_peer(by))
        for by in range(1, nz)
    ]

    for copy in cz[1]:
        copy.wait_recv()
    dwg[...] = (dot(hid[...], allo[...], (0, 0)) * keep[pl.ds(2 * height, height), :].astype(F32)).astype(BF16)

    final = z_out[z]
    for copy, by in zip(dz, range(1, nz)):
        copy.wait_recv()
        final = final + z_in[by]
    ig[...] = final.astype(BF16)

    for copy in started:
        copy.wait_send()


def local(dims, tokens, out_grad, gate_weight, up_weight, down_weight, gate_mask, up_mask, down_mask):
    nx, nl, ny, nz, nc = dims
    rows, width = tokens.shape
    height = down_weight.shape[0]
    half = ny * TILE
    dma = pltpu.SemaphoreType.DMA
    vmem = pl.BlockSpec(memory_space=pltpu.VMEM)
    weight = jax.ShapeDtypeStruct((height, width), BF16)
    scratch = [
        pltpu.VMEM((2, nz, rows, width), BF16),
        pltpu.VMEM((2 * half, width), BF16),
        pltpu.VMEM((2 * half, width), BF16),
        pltpu.VMEM((2 * height, width), BF16),
        pltpu.VMEM((height, width), BF16),
        pltpu.VMEM((3 * height, width), BF16),
        pltpu.VMEM((half, 2 * height), BF16),
        pltpu.VMEM((half, 2 * height), BF16),
        pltpu.VMEM((half, height), BF16),
        pltpu.VMEM((half, height), BF16),
        pltpu.VMEM((half, 2 * height), F32),
        pltpu.VMEM((half, height), F32),
        pltpu.VMEM((half, 2 * height), BF16),
        pltpu.VMEM((nx, TILE, 2 * height), BF16),
        pltpu.VMEM((half, height), BF16),
        pltpu.VMEM((nx, TILE, height), BF16),
        pltpu.VMEM((2 * half, 2 * height), BF16),
        pltpu.VMEM((2 * half, height), BF16),
        pltpu.VMEM((half, width), F32),
        pltpu.VMEM((half, width), F32),
        pltpu.VMEM((half, width), F32),
        pltpu.VMEM((half, width), BF16),
        pltpu.VMEM((ny, TILE, width), BF16),
        pltpu.VMEM((nz, rows, width), F32),
        pltpu.VMEM((nz, rows, width), F32),
        dma((2, nz)), dma((2, nz)), dma((2, ny)), dma((2, ny)), dma((2, ny)), dma((2, ny)),
        dma((2,)), dma((2,)), dma((2, nx)), dma((2, nx)),
        dma((2, nx)), dma((2, nx)), dma((2, nx)), dma((2, nx)),
        dma, dma, dma((ny,)), dma((ny,)), dma((nz,)), dma((nz,)),
    ]
    input_grad, gate_wg, up_wg, down_wg = pl.pallas_call(
        functools.partial(kernel, dims),
        out_shape=(jax.ShapeDtypeStruct((rows, width), BF16), weight, weight, weight),
        in_specs=[vmem] * 8,
        out_specs=(vmem,) * 4,
        scratch_shapes=scratch,
        compiler_params=pltpu.CompilerParams(
            collective_id=0, has_side_effects=True, vmem_limit_bytes=40 * 1024 * 1024
        ),
        name="block",
    )(
        tokens, out_grad, gate_weight.T, up_weight.T, down_weight,
        gate_mask, up_mask, down_mask.T,
    )
    return input_grad, gate_wg.T, up_wg.T, down_wg


def solution(mesh, dims=(8, 2, 8, 4, 2)):
    in_specs = (
        P("col", "row"),
        P("col", "row"),
        P("row", "col"),
        P("row", "col"),
        P("col", "row"),
        P("row", "col"),
        P("row", "col"),
        P("col", "row"),
    )
    out_specs = (P("col", "row"), P("row", "col"), P("row", "col"), P("col", "row"))
    return jax.shard_map(
        functools.partial(local, dims), mesh=mesh, in_specs=in_specs, out_specs=out_specs, check_vma=False
    )
```

```python
import functools

import jax
import jax.numpy as jnp
from jax import lax
from jax.experimental import pallas as pl
from jax.experimental.pallas import tpu as pltpu
from jax.sharding import PartitionSpec as P

F32 = jnp.float32
BF16 = jnp.bfloat16
MESH = pl.DeviceIdType.MESH
TILE = 16


def dot(left, right, at):
    return lax.dot_general(
        left, right, (((at[0],), (at[1],)), ((), ())), preferred_element_type=F32
    )


def orderings(code):
    def step(value, bound):
        return (value >= bound).astype(jnp.int32)

    p0 = step(code, 6) + step(code, 12) + step(code, 18)
    rest = code - 6 * p0
    rank1 = step(rest, 2) + step(rest, 4)
    rank2 = rest - 2 * rank1
    p1 = rank1 + (rank1 >= p0).astype(jnp.int32)
    low, high = jnp.minimum(p0, p1), jnp.maximum(p0, p1)
    rest_low = jnp.where(low > 0, 0, jnp.where(high > 1, 1, 2))
    rest_high = 6 - low - high - rest_low
    p2 = jnp.where(rank2 == 0, rest_low, rest_high)
    return p0, p1, p2, 6 - p0 - p1 - p2


def nibbles(code, bits_are_columns):
    p = orderings(code)
    one = jnp.ones_like(code)
    kept = []
    for at in range(4):
        if bits_are_columns:
            kept.append((one << p[at]) | (one << p[(at + 1) % 4]))
        else:
            bits = jnp.zeros_like(code)
            for i in range(4):
                hit = (p[i] == at) | (p[(i + 1) % 4] == at)
                bits = bits | jnp.where(hit, 1 << i, 0)
            kept.append(bits)
    return [k.astype(F32).astype(BF16) for k in kept]


def expanded(code, bits_are_columns, width, height):
    quarter = width // 4
    parts = nibbles(code, bits_are_columns)
    wide = jnp.zeros((code.shape[1], width), F32)
    d = lax.broadcasted_iota(jnp.int32, (quarter, width), 1)
    a = lax.broadcasted_iota(jnp.int32, (quarter, width), 0)
    for i in range(4):
        spread = (d == 4 * a + i).astype(F32).astype(BF16)
        wide = wide + dot(parts[i], spread, (0, 0))
    f = lax.broadcasted_iota(jnp.int32, (height, height // 4), 0)
    b = lax.broadcasted_iota(jnp.int32, (height, height // 4), 1)
    tall = dot(((f >> 2) == b).astype(F32).astype(BF16), wide.astype(BF16), (1, 0))
    local = lax.broadcasted_iota(jnp.int32, (height, width), 0) & 3
    return ((tall.astype(jnp.int32) >> local) & 1).astype(F32)


def routes(n):
    if n < 4:
        return list(range(1, n)), {}
    if n == 4:
        return [1, 3], {1: [2]}
    return [2, 6, 1, 7], {2: [3, 4], 6: [5]}


def kernel(
    dims,
    tok, og, gw, uw, dw, gm, um, dm,
    ig, gwg, uwg, dwg,
    zin, allt, allo, wcat, wdown, keep, codes,
    zl_gu_out, zl_gu_in, zl_b_out, zl_b_in, sum_gu, sum_b,
    x_gu_out, x_gu_in, x_b_out, x_b_in, gu, hid,
    core_out, core_in, own, y_out, y_in, z_out, z_in,
    load, sent, az_r, ay_r, ac_r, bz_r, bx_r, cx_r, cz_r, d_r,
):
    nx, nl, ny, nz, nc = dims
    row, col = lax.axis_index("row"), lax.axis_index("col")
    x, zl = row // nl, row % nl
    core = col % nc
    z = (col // nc) % nz
    y = col // (nc * nz)
    hand = 1 - 2 * core
    height, width = dw.shape
    rows = tok.shape[0]
    half = ny * TILE

    def x_peer(by):
        return (lax.rem(x + nx + by, nx) * nl + zl, col)

    def y_peer(by):
        return (row, (lax.rem(y + ny + by, ny) * nz + z) * nc + core)

    def z_peer(by):
        return (row, (y * nz + lax.rem(z + by, nz)) * nc + core)

    zl_peer = (x * nl + (1 - zl), col)
    core_peer = (row, (y * nz + z) * nc + (1 - core))

    peers = [y_peer(by) for by in range(1, ny)] + [x_peer(by) for by in range(1, nx)]
    peers += [z_peer(by) for by in range(1, nz)] + [zl_peer, core_peer]
    barrier = pltpu.get_barrier_semaphore()
    for peer in peers:
        pl.semaphore_signal(barrier, inc=1, device_id=peer, device_id_type=MESH)

    loads = [
        pltpu.make_async_copy(src, dst, load.at[i])
        for i, (src, dst) in enumerate(
            (
                (gm, codes.at[0]),
                (gw, wcat.at[pl.ds(0, height), :]),
                (um, codes.at[1]),
                (uw, wcat.at[pl.ds(height, height), :]),
                (dm, codes.at[2]),
                (dw, wdown),
                (tok, zin.at[0, z]),
                (og, zin.at[1, z]),
            )
        )
    ]
    for copy in loads:
        copy.start()

    def send(src, dst, s, r, peer):
        pltpu.make_async_remote_copy(
            src_ref=src, dst_ref=dst, send_sem=s, recv_sem=r,
            device_id=peer, device_id_type=MESH,
        ).start()

    def settle(ref, semaphore):
        pltpu.make_async_copy(ref, ref, semaphore).wait()

    def block(at):
        return pl.ds(pl.multiple_of(at * TILE, TILE), TILE)

    def part(at):
        return pl.ds(pl.multiple_of(at * half, half), half)

    def far_first(n):
        return sorted(range(1, n), key=lambda by: -min(by, n - by))

    def spread(full, base, me, n, peer, s, r, f_r, f_peer):
        direct, relays = routes(n)

        def rows_of(at):
            return full.at[block(base + at), :]

        def first():
            mine = rows_of(me)
            for by in direct:
                send(mine, mine, s, r.at[by], peer(hand * by))
            send(mine, mine, s, f_r, f_peer)

        def take(offsets):
            for by in offsets:
                there = rows_of(lax.rem(me + n * n - hand * by, n))
                settle(there, r.at[by])
                for onward in relays.get(by, []):
                    send(there, there, s, r.at[onward], peer(hand * (onward - by)))
                send(there, there, s, f_r, f_peer)

        def rest():
            settle(full.at[pl.ds(0, half), :], f_r)

        def drained():
            settle(full.at[pl.ds(0, (2 * n - 1) * TILE), :], s)

        via = [by for by in direct if by in relays]
        near = [by for by in direct if by not in relays]
        far = [by for by in range(1, n) if by not in direct]
        return first, take, rest, drained, (via, near, sorted(far, key=lambda by: min(by, n - by)))

    def prepared(i, dst, at):
        kept = expanded(codes[i], i < 2, width, height)
        keep[pl.ds(i * height, height), :] = kept.astype(BF16)
        dst[at, :] = (dst[at, :].astype(F32) * kept).astype(BF16)

    pl.semaphore_wait(barrier, len(peers))

    for k, ref in enumerate((tok, og)):
        for by in range(1, nz):
            send(ref, zin.at[k, z], sent.at[k], az_r.at[k], z_peer(by))

    loads[0].wait()
    loads[1].wait()
    prepared(0, wcat, pl.ds(0, height))
    loads[2].wait()
    loads[3].wait()
    prepared(1, wcat, pl.ds(height, height))

    t_first, t_take, t_rest, t_drained, t_at = spread(
        allt, core * ny, y, ny, y_peer, sent.at[2], ay_r.at[0], ac_r.at[0], core_peer
    )
    o_first, o_take, o_rest, o_drained, o_at = spread(
        allo, core * ny, y, ny, y_peer, sent.at[3], ay_r.at[1], ac_r.at[1], core_peer
    )
    for k, (full, first) in enumerate(((allt, t_first), (allo, o_first))):
        loads[6 + k].wait()
        if nz > 1:
            settle(zin.at[k, pl.ds(0, nz - 1)], az_r.at[k])
        gathered = jnp.concatenate([zin[k, i].astype(F32) for i in range(nz)], axis=0)
        full[block(core * ny + y), :] = gathered.astype(BF16)
        first()

    loads[4].wait()
    loads[5].wait()
    prepared(2, wdown, pl.ds(0, height))

    t_take(t_at[0])
    t_take(t_at[1])
    o_take(o_at[0])
    t_take(t_at[2])
    t_rest()

    def owed(total, out, into, k, full, weight):
        out[...] = dot(full[part(1 - zl), :], weight[...], (1, 1)).astype(BF16)
        for by in far_first(nx) + [0]:
            there = block(lax.rem(x + by, nx))
            send(out.at[there, :], into.at[there, :], sent.at[4 + k], bz_r.at[k, by], zl_peer)
        total[...] = dot(full[part(zl), :], weight[...], (1, 1))

    owed(sum_gu, zl_gu_out, zl_gu_in, 0, allt, wcat)
    o_take(o_at[1])
    o_take(o_at[2])
    o_rest()
    owed(sum_b, zl_b_out, zl_b_in, 1, allo, wdown)

    parts = ((sum_gu, zl_gu_in, x_gu_out, x_gu_in), (sum_b, zl_b_in, x_b_out, x_b_in))
    for k, (total, arrived, out, into) in enumerate(parts):
        for by in far_first(nx):
            there = block(lax.rem(x + by, nx))
            settle(arrived.at[there, :], bz_r.at[k, by])
            out[there, :] = (total[there, :] + arrived[there, :].astype(F32)).astype(BF16)
            send(out.at[there, :], into.at[by], sent.at[6 + k], bx_r.at[k], x_peer(by))

    sums = []
    for k, (total, arrived, out, into) in enumerate(parts):
        here = block(x)
        settle(arrived.at[here, :], bz_r.at[k, 0])
        value = total[here, :] + arrived[here, :].astype(F32)
        settle(into.at[pl.ds(1, nx - 1)], bx_r.at[k])
        for by in range(1, nx):
            value = value + into[by].astype(F32)
        sums.append(value)

    gate, up, back = sums[0][:, :height], sums[0][:, height:], sums[1]
    logistic = 1.0 / (1.0 + jnp.exp(-gate))
    swish = gate * logistic
    up_grad = back * swish
    gate_grad = back * up * logistic * (1.0 + gate * (1.0 - logistic))
    mine = block(zl * nx + x)
    gu[mine, :] = jnp.concatenate([gate_grad, up_grad], axis=1).astype(BF16)
    g_first, g_take, g_rest, g_drained, g_at = spread(
        gu, zl * nx, x, nx, x_peer, sent.at[8], cx_r.at[0], cz_r.at[0], zl_peer
    )
    h_first, h_take, h_rest, h_drained, h_at = spread(
        hid, zl * nx, x, nx, x_peer, sent.at[9], cx_r.at[1], cz_r.at[1], zl_peer
    )
    g_first()
    hid[mine, :] = (swish * up).astype(BF16)
    g_take(g_at[0])
    h_first()
    g_take(g_at[1])
    g_take(g_at[2])
    h_take(h_at[0])
    g_rest()

    core_out[...] = dot(gu[part(1 - core), :], wcat[...], (1, 0))
    send(core_out, core_in, sent.at[10], d_r.at[0], core_peer)
    own[...] = dot(gu[part(core), :], wcat[...], (1, 0))
    h_take(h_at[1])
    settle(core_in, d_r.at[0])
    total = own[...] + core_in[...]
    own[...] = total
    y_out[...] = total.astype(BF16)
    for by in far_first(ny):
        send(y_out.at[block(lax.rem(y + by, ny)), :], y_in.at[by], sent.at[11], d_r.at[1], y_peer(by))
    h_take(h_at[2])

    gwg[...] = (dot(gu[:, :height], allt[...], (0, 0)) * keep[pl.ds(0, height), :].astype(F32)).astype(BF16)
    uwg[...] = (dot(gu[:, height:], allt[...], (0, 0)) * keep[pl.ds(height, height), :].astype(F32)).astype(BF16)
    h_rest()

    value = own[block(y), :]
    settle(y_in.at[pl.ds(1, ny - 1)], d_r.at[1])
    for by in range(1, ny):
        value = value + y_in[by].astype(F32)
    for i in range(nz):
        z_out[i] = value[i * rows : (i + 1) * rows, :]
    for by in range(1, nz):
        send(z_out.at[lax.rem(z + by, nz)], z_in.at[by], sent.at[12], d_r.at[2], z_peer(by))

    dwg[...] = (dot(hid[...], allo[...], (0, 0)) * keep[pl.ds(2 * height, height), :].astype(F32)).astype(BF16)
    for k in range(2):
        if nz > 1:
            settle(zin.at[k, pl.ds(0, nz - 1)], sent.at[k])
    for drained in (t_drained, o_drained, g_drained, h_drained):
        drained()
    settle(zl_gu_out, sent.at[4])
    settle(zl_b_out, sent.at[5])
    settle(x_gu_out.at[pl.ds(0, (nx - 1) * TILE), :], sent.at[6])
    settle(x_b_out.at[pl.ds(0, (nx - 1) * TILE), :], sent.at[7])
    settle(core_out, sent.at[10])
    settle(y_out.at[pl.ds(0, (ny - 1) * TILE), :], sent.at[11])

    final = z_out[z]
    if nz > 1:
        settle(z_in.at[pl.ds(1, nz - 1)], d_r.at[2])
    for by in range(1, nz):
        final = final + z_in[by]
    ig[...] = final.astype(BF16)
    if nz > 1:
        settle(z_out.at[pl.ds(0, nz - 1)], sent.at[12])


def written(*refs):
    done = refs[-1]
    copies = [
        pltpu.make_async_copy(refs[i], refs[i + 4], done.at[i]) for i in range(4)
    ]
    for copy in copies:
        copy.start()
    for copy in copies:
        copy.wait()


def local(dims, tokens, out_grad, gate_weight, up_weight, down_weight, gate_mask, up_mask, down_mask):
    nx, nl, ny, nz, nc = dims
    rows, width = tokens.shape
    height = down_weight.shape[0]
    half = ny * TILE
    dma = pltpu.SemaphoreType.DMA
    vmem = pl.BlockSpec(memory_space=pltpu.VMEM)
    weight = jax.ShapeDtypeStruct((height, width), BF16)
    scratch = [
        pltpu.VMEM((2, nz, rows, width), BF16),
        pltpu.VMEM((2 * half, width), BF16),
        pltpu.VMEM((2 * half, width), BF16),
        pltpu.VMEM((2 * height, width), BF16),
        pltpu.VMEM((height, width), BF16),
        pltpu.VMEM((3 * height, width), BF16),
        pltpu.VMEM((3, width // 4, height // 4), jnp.int32),
        pltpu.VMEM((half, 2 * height), BF16),
        pltpu.VMEM((half, 2 * height), BF16),
        pltpu.VMEM((half, height), BF16),
        pltpu.VMEM((half, height), BF16),
        pltpu.VMEM((half, 2 * height), F32),
        pltpu.VMEM((half, height), F32),
        pltpu.VMEM((half, 2 * height), BF16),
        pltpu.VMEM((nx, TILE, 2 * height), BF16),
        pltpu.VMEM((half, height), BF16),
        pltpu.VMEM((nx, TILE, height), BF16),
        pltpu.VMEM((2 * half, 2 * height), BF16),
        pltpu.VMEM((2 * half, height), BF16),
        pltpu.VMEM((half, width), F32),
        pltpu.VMEM((half, width), F32),
        pltpu.VMEM((half, width), F32),
        pltpu.VMEM((half, width), BF16),
        pltpu.VMEM((ny, TILE, width), BF16),
        pltpu.VMEM((nz, rows, width), F32),
        pltpu.VMEM((nz, rows, width), F32),
        dma((8,)), dma((13,)), dma((2,)), dma((2, ny)), dma((2,)),
        dma((2, nx)), dma((2,)), dma((2, nx)), dma((2,)), dma((3,)),
    ]
    held = (jax.ShapeDtypeStruct((rows, width), BF16), weight, weight, weight)
    results = pl.pallas_call(
        functools.partial(kernel, dims),
        out_shape=held,
        in_specs=[pl.BlockSpec(memory_space=pltpu.HBM)] * 8,
        out_specs=(vmem,) * 4,
        scratch_shapes=scratch,
        compiler_params=pltpu.CompilerParams(
            collective_id=0, has_side_effects=True, vmem_limit_bytes=40 * 1024 * 1024
        ),
        name="block",
    )(
        *(
            pltpu.with_memory_space_constraint(a, pltpu.HBM)
            for a in (
                tokens, out_grad, gate_weight.T, up_weight.T, down_weight,
                gate_mask, up_mask, down_mask.T,
            )
        )
    )
    input_grad, gate_wg, up_wg, down_wg = pl.pallas_call(
        written,
        out_shape=held,
        in_specs=[pl.BlockSpec(memory_space=pl.ANY)] * 4,
        out_specs=(pl.BlockSpec(memory_space=pl.ANY),) * 4,
        scratch_shapes=[dma((4,))],
        compiler_params=pltpu.CompilerParams(vmem_limit_bytes=2 * 1024 * 1024),
        name="write",
    )(*results)
    return input_grad, gate_wg.T, up_wg.T, down_wg


def solution(mesh, dims=(8, 2, 8, 4, 2)):
    in_specs = (
        P("col", "row"),
        P("col", "row"),
        P("row", "col"),
        P("row", "col"),
        P("col", "row"),
        P("row", "col"),
        P("row", "col"),
        P("col", "row"),
    )
    out_specs = (P("col", "row"), P("row", "col"), P("row", "col"), P("col", "row"))
    return jax.shard_map(
        functools.partial(local, dims), mesh=mesh, in_specs=in_specs, out_specs=out_specs, check_vma=False
    )
```

```python
import functools

import jax
import jax.numpy as jnp
from jax import lax
from jax.experimental import pallas as pl
from jax.experimental.pallas import tpu as pltpu
from jax.sharding import PartitionSpec as P

F32 = jnp.float32
BF16 = jnp.bfloat16
MESH = pl.DeviceIdType.MESH
TILE = 16


def dot(left, right, at):
    return lax.dot_general(
        left, right, (((at[0],), (at[1],)), ((), ())), preferred_element_type=F32
    )


def orderings(code):
    def step(value, bound):
        return (value >= bound).astype(jnp.int32)

    p0 = step(code, 6) + step(code, 12) + step(code, 18)
    rest = code - 6 * p0
    rank1 = step(rest, 2) + step(rest, 4)
    rank2 = rest - 2 * rank1
    p1 = rank1 + (rank1 >= p0).astype(jnp.int32)
    low, high = jnp.minimum(p0, p1), jnp.maximum(p0, p1)
    rest_low = jnp.where(low > 0, 0, jnp.where(high > 1, 1, 2))
    rest_high = 6 - low - high - rest_low
    p2 = jnp.where(rank2 == 0, rest_low, rest_high)
    return p0, p1, p2, 6 - p0 - p1 - p2


def nibbles(code, bits_are_columns):
    p = orderings(code)
    one = jnp.ones_like(code)
    kept = []
    for at in range(4):
        if bits_are_columns:
            kept.append((one << p[at]) | (one << p[(at + 1) % 4]))
        else:
            bits = jnp.zeros_like(code)
            for i in range(4):
                hit = (p[i] == at) | (p[(i + 1) % 4] == at)
                bits = bits | jnp.where(hit, 1 << i, 0)
            kept.append(bits)
    return [k.astype(F32).astype(BF16) for k in kept]


def expanded(code, bits_are_columns, width, height):
    quarter = width // 4
    parts = nibbles(code, bits_are_columns)
    wide = jnp.zeros((code.shape[1], width), F32)
    d = lax.broadcasted_iota(jnp.int32, (quarter, width), 1)
    a = lax.broadcasted_iota(jnp.int32, (quarter, width), 0)
    for i in range(4):
        spread = (d == 4 * a + i).astype(F32).astype(BF16)
        wide = wide + dot(parts[i], spread, (0, 0))
    f = lax.broadcasted_iota(jnp.int32, (height, height // 4), 0)
    b = lax.broadcasted_iota(jnp.int32, (height, height // 4), 1)
    tall = dot(((f >> 2) == b).astype(F32).astype(BF16), wide.astype(BF16), (1, 0))
    local = lax.broadcasted_iota(jnp.int32, (height, width), 0) & 3
    return ((tall.astype(jnp.int32) >> local) & 1).astype(F32)


def routes(n):
    if n < 4:
        return list(range(1, n)), {}
    if n == 4:
        return [1, 3], {1: [2]}
    return [2, 6, 1, 7], {2: [3, 4], 6: [5]}


def kernel(
    dims,
    tok, og, gw, uw, dw, gm, um, dm,
    ig, gwg, uwg, dwg,
    zin, allt, allo, wcat, wdown, keep, codes,
    zl_gu_out, zl_gu_in, zl_b_out, zl_b_in, sum_gu, sum_b,
    x_gu_out, x_gu_in, x_b_out, x_b_in, gu, hid,
    core_out, core_in, own, y_out, y_in, z_out, z_in,
    load, sent, az_r, ay_r, ac_r, bz_r, bx_r, cx_r, cz_r, d_r,
):
    nx, nl, ny, nz, nc = dims
    row, col = lax.axis_index("row"), lax.axis_index("col")
    x, zl = row // nl, row % nl
    core = col % nc
    z = (col // nc) % nz
    y = col // (nc * nz)
    hand = 1 - 2 * core
    height, width = dw.shape
    width_of = (sum_gu.shape[1], sum_b.shape[1])
    rows = tok.shape[0]
    half = ny * TILE

    def x_peer(by):
        return (lax.rem(x + nx + by, nx) * nl + zl, col)

    def y_peer(by):
        return (row, (lax.rem(y + ny + by, ny) * nz + z) * nc + core)

    def z_peer(by):
        return (row, (y * nz + lax.rem(z + by, nz)) * nc + core)

    zl_peer = (x * nl + (1 - zl), col)
    core_peer = (row, (y * nz + z) * nc + (1 - core))

    peers = [y_peer(by) for by in range(1, ny)] + [x_peer(by) for by in range(1, nx)]
    peers += [z_peer(by) for by in range(1, nz)] + [zl_peer, core_peer]
    barrier = pltpu.get_barrier_semaphore()
    for peer in peers:
        pl.semaphore_signal(barrier, inc=1, device_id=peer, device_id_type=MESH)

    loads = [
        pltpu.make_async_copy(src, dst, load.at[i])
        for i, (src, dst) in enumerate(
            (
                (gm, codes.at[0]),
                (gw, wcat.at[pl.ds(0, height), :]),
                (um, codes.at[1]),
                (uw, wcat.at[pl.ds(height, height), :]),
                (dm, codes.at[2]),
                (dw, wdown),
                (tok, zin.at[0, z]),
                (og, zin.at[1, z]),
            )
        )
    ]
    for copy in loads:
        copy.start()

    def send(src, dst, s, r, peer):
        pltpu.make_async_remote_copy(
            src_ref=src, dst_ref=dst, send_sem=s, recv_sem=r,
            device_id=peer, device_id_type=MESH,
        ).start()

    def settle(ref, semaphore):
        pltpu.make_async_copy(ref, ref, semaphore).wait()

    def block(at):
        return pl.ds(pl.multiple_of(at * TILE, TILE), TILE)

    def part(at):
        return pl.ds(pl.multiple_of(at * half, half), half)

    def far_first(n):
        return sorted(range(1, n), key=lambda by: -min(by, n - by))

    def spread(full, base, me, n, peer, s, r, f_r, f_peer, straight=False):
        direct, relays = routes(n)

        def rows_of(at):
            return full.at[block(base + at), :]

        def first():
            mine = rows_of(me)
            for by in direct:
                send(mine, mine, s, r.at[by], peer(hand * by))
            send(mine, mine, s, f_r.at[0], f_peer)
            if straight:

                @pl.when(core == 0)
                def _():
                    for by in far_first(n):
                        if by not in direct:
                            send(mine, mine, s, r.at[by], peer(hand * by))


        def take(offsets):
            for by in offsets:
                there = rows_of(lax.rem(me + n * n - hand * by, n))
                settle(there, r.at[by])
                if by in relays:

                    def onwards():
                        for onward in relays[by]:
                            send(there, there, s, r.at[onward], peer(hand * (onward - by)))

                    if straight:
                        pl.when(core == 1)(onwards)
                    else:
                        onwards()
                send(there, there, s, f_r.at[0 if by in direct else 1], f_peer)

        def rest_near():
            settle(full.at[pl.ds(0, (1 + len(direct)) * TILE), :], f_r.at[0])

        def rest_far():
            if len(direct) + 1 < n:
                settle(full.at[pl.ds(0, (n - 1 - len(direct)) * TILE), :], f_r.at[1])

        def rest():
            rest_near()
            rest_far()

        def drained():
            settle(full.at[pl.ds(0, (2 * n - 1) * TILE), :], s)

        via = [by for by in direct if by in relays]
        near = [by for by in direct if by not in relays]
        far = [by for by in range(1, n) if by not in direct]
        return first, take, (rest, rest_near, rest_far), drained, (via, near, sorted(far, key=lambda by: min(by, n - by)))

    def prepared(i, dst, at):
        kept = expanded(codes[i], i < 2, width, height)
        keep[pl.ds(i * height, height), :] = kept.astype(BF16)
        dst[at, :] = (dst[at, :].astype(F32) * kept).astype(BF16)

    pl.semaphore_wait(barrier, len(peers))

    for k, ref in enumerate((tok, og)):
        for by in range(1, nz):
            send(ref, zin.at[k, z], sent.at[k], az_r.at[k], z_peer(by))

    loads[0].wait()
    loads[1].wait()
    prepared(0, wcat, pl.ds(0, height))
    loads[2].wait()
    loads[3].wait()
    prepared(1, wcat, pl.ds(height, height))

    t_first, t_take, (_, t_rest_near, t_rest_far), t_drained, t_at = spread(
        allt, core * ny, y, ny, y_peer, sent.at[2], ay_r.at[0], ac_r.at[0], core_peer
    )
    o_first, o_take, (o_rest, _, _), o_drained, o_at = spread(
        allo, core * ny, y, ny, y_peer, sent.at[3], ay_r.at[1], ac_r.at[1], core_peer
    )
    for k, full in enumerate((allt, allo)):
        loads[6 + k].wait()
        if nz > 1:
            settle(zin.at[k, pl.ds(0, nz - 1)], az_r.at[k])
        gathered = jnp.concatenate([zin[k, i].astype(F32) for i in range(nz)], axis=0)
        full[block(core * ny + y), :] = gathered.astype(BF16)
        (t_first, o_first)[k]()

    loads[4].wait()
    loads[5].wait()
    prepared(2, wdown, pl.ds(0, height))

    t_take(t_at[0])
    t_take(t_at[1])
    o_take(o_at[0])

    split = width_of[0]
    parts = ((sum_gu, zl_gu_out, zl_gu_in, x_gu_out, x_gu_in), (sum_b, zl_b_out, zl_b_in, x_b_out, x_b_in))

    def early(offsets):
        spots = [lax.rem(y + by, ny) for by in offsets]
        left = jnp.concatenate([allt[block((1 - zl) * ny + at), :] for at in spots], axis=0)
        product = dot(left, wcat[pl.ds(0, split), :], (1, 1)).astype(BF16)
        for i, at in enumerate(spots):
            zl_gu_out[block(at), :] = product[i * TILE : (i + 1) * TILE, :]
            send(zl_gu_out.at[block(at), :], zl_gu_in.at[block(at), :], sent.at[4], bz_r.at[0, at], zl_peer)

    def late(at):
        back = dot(allo[at, :], wdown[...], (1, 1))
        tail = dot(allt[at, :], wcat[pl.ds(split, 2 * height - split), :], (1, 1))
        return jnp.concatenate([back, tail], axis=1)

    def pair(k, at):
        total, _, arrived, out, _ = parts[k]
        there = block(at)
        settle(arrived.at[there, :], bz_r.at[k, at])
        out[there, :] = (total[there, :] + arrived[there, :].astype(F32)).astype(BF16)

    def pass_on(k, at, by):
        out, into = parts[k][3:]
        send(out.at[block(at), :], into.at[by], sent.at[6 + k], bx_r.at[k], (at * nl + zl, col))

    near = [0] + routes(ny)[0]
    distant = [by for by in range(1, ny) if by not in near]
    t_rest_near()
    early(near)
    t_take(t_at[2])
    t_rest_far()
    if distant:
        early(distant)
    sum_gu[...] = dot(allt[part(zl), :], wcat[pl.ds(0, split), :], (1, 1))

    def gu_pairs(offsets):
        for by in offsets:
            at = lax.rem(y + by, ny)
            pair(0, at)

            @pl.when(at != x)
            def _():
                pass_on(0, at, lax.rem(at + nx - x, nx))

    gu_pairs(near)
    o_take(o_at[1])
    o_take(o_at[2])
    o_rest()
    zl_b_out[...] = late(part(1 - zl)).astype(BF16)
    for by in far_first(nx) + [0]:
        at = lax.rem(x + by, nx)
        send(zl_b_out.at[block(at), :], zl_b_in.at[block(at), :], sent.at[5], bz_r.at[1, at], zl_peer)
    sum_b[...] = late(part(zl))
    gu_pairs(distant)
    for by in far_first(nx):
        at = lax.rem(x + by, nx)
        pair(1, at)
        pass_on(1, at, by)
    settle(zl_b_in.at[block(x), :], bz_r.at[1, x])

    sums = []
    for k, (total, _, arrived, out, into) in enumerate(parts):
        here = block(x)
        value = total[here, :] + arrived[here, :].astype(F32)
        settle(into.at[pl.ds(1, nx - 1)], bx_r.at[k])
        for by in range(1, nx):
            value = value + into[by].astype(F32)
        sums.append(value)

    gate, back = sums[0][:, :height], sums[1][:, :height]
    up = jnp.concatenate([sums[0][:, height:], sums[1][:, height:]], axis=1)
    logistic = 1.0 / (1.0 + jnp.exp(-gate))
    swish = gate * logistic
    up_grad = back * swish
    gate_grad = back * up * logistic * (1.0 + gate * (1.0 - logistic))
    mine = block(zl * nx + x)
    gu[mine, :] = jnp.concatenate([gate_grad, up_grad], axis=1).astype(BF16)
    g_first, g_take, (g_rest, _, _), g_drained, g_at = spread(
        gu, zl * nx, x, nx, x_peer, sent.at[8], cx_r.at[0], cz_r.at[0], zl_peer, straight=True
    )
    h_first, h_take, (h_rest, _, _), h_drained, h_at = spread(
        hid, zl * nx, x, nx, x_peer, sent.at[9], cx_r.at[1], cz_r.at[1], zl_peer
    )
    g_first()
    hid[mine, :] = (swish * up).astype(BF16)
    g_take(g_at[0])
    h_first()
    g_take(g_at[1])
    g_take(g_at[2])
    g_rest()

    core_out[...] = dot(gu[part(1 - core), :], wcat[...], (1, 0))
    send(core_out, core_in, sent.at[10], d_r.at[0], core_peer)
    own[...] = dot(gu[part(core), :], wcat[...], (1, 0))
    settle(core_in, d_r.at[0])
    total = own[...] + core_in[...]
    own[...] = total
    y_out[...] = total.astype(BF16)
    for by in far_first(ny):
        send(y_out.at[block(lax.rem(y + by, ny)), :], y_in.at[by], sent.at[11], d_r.at[1], y_peer(by))
    h_take(h_at[0])
    h_take(h_at[1])

    gwg[...] = (dot(gu[:, :height], allt[...], (0, 0)) * keep[pl.ds(0, height), :].astype(F32)).astype(BF16)
    uwg[...] = (dot(gu[:, height:], allt[...], (0, 0)) * keep[pl.ds(height, height), :].astype(F32)).astype(BF16)

    h_take(h_at[2])
    value = own[block(y), :]
    settle(y_in.at[pl.ds(1, ny - 1)], d_r.at[1])
    for by in range(1, ny):
        value = value + y_in[by].astype(F32)
    for i in range(nz):
        z_out[i] = value[i * rows : (i + 1) * rows, :]
    for by in range(1, nz):
        send(z_out.at[lax.rem(z + by, nz)], z_in.at[by], sent.at[12], d_r.at[2], z_peer(by))

    h_rest()
    dwg[...] = (dot(hid[...], allo[...], (0, 0)) * keep[pl.ds(2 * height, height), :].astype(F32)).astype(BF16)
    for k in range(2):
        if nz > 1:
            settle(zin.at[k, pl.ds(0, nz - 1)], sent.at[k])
    for drained in (t_drained, o_drained, g_drained, h_drained):
        drained()
    settle(zl_gu_out, sent.at[4])
    settle(zl_b_out, sent.at[5])
    settle(x_gu_out.at[pl.ds(0, (nx - 1) * TILE), :], sent.at[6])
    settle(x_b_out.at[pl.ds(0, (nx - 1) * TILE), :], sent.at[7])
    settle(core_out, sent.at[10])
    settle(y_out.at[pl.ds(0, (ny - 1) * TILE), :], sent.at[11])

    final = z_out[z]
    if nz > 1:
        settle(z_in.at[pl.ds(1, nz - 1)], d_r.at[2])
    for by in range(1, nz):
        final = final + z_in[by]
    ig[...] = final.astype(BF16)
    if nz > 1:
        settle(z_out.at[pl.ds(0, nz - 1)], sent.at[12])


def written(*refs):
    done = refs[-1]
    copies = [
        pltpu.make_async_copy(refs[i], refs[i + 4], done.at[i]) for i in range(4)
    ]
    for copy in copies:
        copy.start()
    for copy in copies:
        copy.wait()


def local(dims, tokens, out_grad, gate_weight, up_weight, down_weight, gate_mask, up_mask, down_mask):
    nx, nl, ny, nz, nc = dims
    rows, width = tokens.shape
    height = down_weight.shape[0]
    half = ny * TILE
    lead = 2 * height // 128 * 128
    lag = 3 * height - lead
    dma = pltpu.SemaphoreType.DMA
    vmem = pl.BlockSpec(memory_space=pltpu.VMEM)
    weight = jax.ShapeDtypeStruct((height, width), BF16)
    scratch = [
        pltpu.VMEM((2, nz, rows, width), BF16),
        pltpu.VMEM((2 * half, width), BF16),
        pltpu.VMEM((2 * half, width), BF16),
        pltpu.VMEM((2 * height, width), BF16),
        pltpu.VMEM((height, width), BF16),
        pltpu.VMEM((3 * height, width), BF16),
        pltpu.VMEM((3, width // 4, height // 4), jnp.int32),
        pltpu.VMEM((half, lead), BF16),
        pltpu.VMEM((half, lead), BF16),
        pltpu.VMEM((half, lag), BF16),
        pltpu.VMEM((half, lag), BF16),
        pltpu.VMEM((half, lead), F32),
        pltpu.VMEM((half, lag), F32),
        pltpu.VMEM((half, lead), BF16),
        pltpu.VMEM((nx, TILE, lead), BF16),
        pltpu.VMEM((half, lag), BF16),
        pltpu.VMEM((nx, TILE, lag), BF16),
        pltpu.VMEM((2 * half, 2 * height), BF16),
        pltpu.VMEM((2 * half, height), BF16),
        pltpu.VMEM((half, width), F32),
        pltpu.VMEM((half, width), F32),
        pltpu.VMEM((half, width), F32),
        pltpu.VMEM((half, width), BF16),
        pltpu.VMEM((ny, TILE, width), BF16),
        pltpu.VMEM((nz, rows, width), F32),
        pltpu.VMEM((nz, rows, width), F32),
        dma((8,)), dma((13,)), dma((2,)), dma((2, ny)), dma((2, 2)),
        dma((2, nx)), dma((2,)), dma((2, nx)), dma((2, 2)), dma((3,)),
    ]
    held = (jax.ShapeDtypeStruct((rows, width), BF16), weight, weight, weight)
    results = pl.pallas_call(
        functools.partial(kernel, dims),
        out_shape=held,
        in_specs=[pl.BlockSpec(memory_space=pltpu.HBM)] * 8,
        out_specs=(vmem,) * 4,
        scratch_shapes=scratch,
        compiler_params=pltpu.CompilerParams(
            collective_id=0, has_side_effects=True, vmem_limit_bytes=40 * 1024 * 1024
        ),
        name="block",
    )(
        *(
            pltpu.with_memory_space_constraint(a, pltpu.HBM)
            for a in (
                tokens, out_grad, gate_weight.T, up_weight.T, down_weight,
                gate_mask, up_mask, down_mask.T,
            )
        )
    )
    input_grad, gate_wg, up_wg, down_wg = pl.pallas_call(
        written,
        out_shape=held,
        in_specs=[pl.BlockSpec(memory_space=pl.ANY)] * 4,
        out_specs=(pl.BlockSpec(memory_space=pl.ANY),) * 4,
        scratch_shapes=[dma((4,))],
        compiler_params=pltpu.CompilerParams(vmem_limit_bytes=2 * 1024 * 1024),
        name="write",
    )(*results)
    return input_grad, gate_wg.T, up_wg.T, down_wg


def solution(mesh, dims=(8, 2, 8, 4, 2)):
    in_specs = (
        P("col", "row"),
        P("col", "row"),
        P("row", "col"),
        P("row", "col"),
        P("col", "row"),
        P("row", "col"),
        P("row", "col"),
        P("col", "row"),
    )
    out_specs = (P("col", "row"), P("row", "col"), P("row", "col"), P("col", "row"))
    return jax.shard_map(
        functools.partial(local, dims), mesh=mesh, in_specs=in_specs, out_specs=out_specs, check_vma=False
    )
```

```python
import functools

import jax
import jax.numpy as jnp
from jax import lax
from jax.experimental import pallas as pl
from jax.experimental.pallas import tpu as pltpu
from jax.sharding import PartitionSpec as P

F32 = jnp.float32
BF16 = jnp.bfloat16
MESH = pl.DeviceIdType.MESH
TILE = 16


def dot(left, right, at):
    return lax.dot_general(
        left, right, (((at[0],), (at[1],)), ((), ())), preferred_element_type=F32
    )


def orderings(code):
    def step(value, bound):
        return (value >= bound).astype(jnp.int32)

    p0 = step(code, 6) + step(code, 12) + step(code, 18)
    rest = code - 6 * p0
    rank1 = step(rest, 2) + step(rest, 4)
    rank2 = rest - 2 * rank1
    p1 = rank1 + (rank1 >= p0).astype(jnp.int32)
    low, high = jnp.minimum(p0, p1), jnp.maximum(p0, p1)
    rest_low = jnp.where(low > 0, 0, jnp.where(high > 1, 1, 2))
    rest_high = 6 - low - high - rest_low
    p2 = jnp.where(rank2 == 0, rest_low, rest_high)
    return p0, p1, p2, 6 - p0 - p1 - p2


def nibbles(code, bits_are_columns):
    p = orderings(code)
    one = jnp.ones_like(code)
    kept = []
    for at in range(4):
        if bits_are_columns:
            kept.append((one << p[at]) | (one << p[(at + 1) % 4]))
        else:
            bits = jnp.zeros_like(code)
            for i in range(4):
                hit = (p[i] == at) | (p[(i + 1) % 4] == at)
                bits = bits | jnp.where(hit, 1 << i, 0)
            kept.append(bits)
    return [k.astype(F32).astype(BF16) for k in kept]


def expanded(code, bits_are_columns, width, height):
    quarter = width // 4
    parts = nibbles(code, bits_are_columns)
    wide = jnp.zeros((code.shape[1], width), F32)
    d = lax.broadcasted_iota(jnp.int32, (quarter, width), 1)
    a = lax.broadcasted_iota(jnp.int32, (quarter, width), 0)
    for i in range(4):
        spread = (d == 4 * a + i).astype(F32).astype(BF16)
        wide = wide + dot(parts[i], spread, (0, 0))
    f = lax.broadcasted_iota(jnp.int32, (height, height // 4), 0)
    b = lax.broadcasted_iota(jnp.int32, (height, height // 4), 1)
    tall = dot(((f >> 2) == b).astype(F32).astype(BF16), wide.astype(BF16), (1, 0))
    local = lax.broadcasted_iota(jnp.int32, (height, width), 0) & 3
    return ((tall.astype(jnp.int32) >> local) & 1).astype(F32)


def routes(n):
    if n < 4:
        return list(range(1, n)), {}
    if n == 4:
        return [1, 3], {1: [2]}
    return [2, 6, 1, 7], {2: [3, 4], 6: [5]}


def kernel(
    dims,
    tok, og, gw, uw, dw, gm, um, dm,
    ig, gwg, uwg, dwg,
    zin, allt, allo, wcat, wdown, keep, codes,
    zl_gu_out, zl_gu_in, zl_b_out, zl_b_in, sum_gu, sum_b,
    x_gu_out, x_gu_in, x_b_out, x_b_in, gu, hid,
    core_out, core_in, own, y_out, y_in, z_out, z_in,
    load, sent, az_r, ay_r, ac_r, bz_r, bx_r, cx_r, cz_r, d_r,
):
    nx, nl, ny, nz, nc = dims
    row, col = lax.axis_index("row"), lax.axis_index("col")
    x, zl = row // nl, row % nl
    core = col % nc
    z = (col // nc) % nz
    y = col // (nc * nz)
    hand = 1 - 2 * core
    height, width = dw.shape
    width_of = (sum_gu.shape[1], sum_b.shape[1])
    rows = tok.shape[0]
    half = ny * TILE

    def x_peer(by):
        return (lax.rem(x + nx + by, nx) * nl + zl, col)

    def y_peer(by):
        return (row, (lax.rem(y + ny + by, ny) * nz + z) * nc + core)

    def z_peer(by):
        return (row, (y * nz + lax.rem(z + by, nz)) * nc + core)

    zl_peer = (x * nl + (1 - zl), col)
    core_peer = (row, (y * nz + z) * nc + (1 - core))

    peers = [y_peer(by) for by in range(1, ny)] + [x_peer(by) for by in range(1, nx)]
    peers += [z_peer(by) for by in range(1, nz)] + [zl_peer, core_peer]
    barrier = pltpu.get_barrier_semaphore()
    for peer in peers:
        pl.semaphore_signal(barrier, inc=1, device_id=peer, device_id_type=MESH)

    loads = [
        pltpu.make_async_copy(src, dst, load.at[i])
        for i, (src, dst) in enumerate(
            (
                (gm, codes.at[0]),
                (gw, wcat.at[pl.ds(0, height), :]),
                (um, codes.at[1]),
                (uw, wcat.at[pl.ds(height, height), :]),
                (dm, codes.at[2]),
                (dw, wdown),
                (tok, zin.at[0, z]),
                (og, zin.at[1, z]),
            )
        )
    ]
    for copy in loads:
        copy.start()

    def send(src, dst, s, r, peer):
        pltpu.make_async_remote_copy(
            src_ref=src, dst_ref=dst, send_sem=s, recv_sem=r,
            device_id=peer, device_id_type=MESH,
        ).start()

    def settle(ref, semaphore):
        pltpu.make_async_copy(ref, ref, semaphore).wait()

    def block(at):
        return pl.ds(pl.multiple_of(at * TILE, TILE), TILE)

    def part(at):
        return pl.ds(pl.multiple_of(at * half, half), half)

    def far_first(n):
        return sorted(range(1, n), key=lambda by: -min(by, n - by))

    def spread(full, base, me, n, peer, s, r, f_r, f_peer, straight=False):
        direct, relays = routes(n)

        def rows_of(at):
            return full.at[block(base + at), :]

        def first():
            mine = rows_of(me)
            for by in direct:
                send(mine, mine, s, r.at[by], peer(hand * by))
            send(mine, mine, s, f_r.at[0], f_peer)
            if straight:

                @pl.when(core == 0)
                def _():
                    for by in far_first(n):
                        if by not in direct:
                            send(mine, mine, s, r.at[by], peer(hand * by))


        def take(offsets):
            for by in offsets:
                there = rows_of(lax.rem(me + n * n - hand * by, n))
                settle(there, r.at[by])
                if by in relays:

                    def onwards():
                        for onward in relays[by]:
                            send(there, there, s, r.at[onward], peer(hand * (onward - by)))

                    if straight:
                        pl.when(core == 1)(onwards)
                    else:
                        onwards()
                send(there, there, s, f_r.at[0 if by in direct else 1], f_peer)

        def rest_near():
            settle(full.at[pl.ds(0, (1 + len(direct)) * TILE), :], f_r.at[0])

        def rest_far():
            if len(direct) + 1 < n:
                settle(full.at[pl.ds(0, (n - 1 - len(direct)) * TILE), :], f_r.at[1])

        def rest():
            rest_near()
            rest_far()

        def drained():
            settle(full.at[pl.ds(0, (2 * n - 1) * TILE), :], s)

        via = [by for by in direct if by in relays]
        near = [by for by in direct if by not in relays]
        far = [by for by in range(1, n) if by not in direct]
        return first, take, (rest, rest_near, rest_far), drained, (via, near, sorted(far, key=lambda by: min(by, n - by)))

    def prepared(i, dst, at):
        kept = expanded(codes[i], i < 2, width, height)
        keep[pl.ds(i * height, height), :] = kept.astype(BF16)
        dst[at, :] = (dst[at, :].astype(F32) * kept).astype(BF16)

    pl.semaphore_wait(barrier, len(peers))

    for k, ref in enumerate((tok, og)):
        for by in range(1, nz):
            send(ref, zin.at[k, z], sent.at[k], az_r.at[k], z_peer(by))

    loads[0].wait()
    loads[1].wait()
    prepared(0, wcat, pl.ds(0, height))
    loads[2].wait()
    loads[3].wait()
    prepared(1, wcat, pl.ds(height, height))

    t_first, t_take, (_, t_rest_near, t_rest_far), t_drained, t_at = spread(
        allt, core * ny, y, ny, y_peer, sent.at[2], ay_r.at[0], ac_r.at[0], core_peer
    )
    o_first, o_take, (_, o_rest_near, o_rest_far), o_drained, o_at = spread(
        allo, core * ny, y, ny, y_peer, sent.at[3], ay_r.at[1], ac_r.at[1], core_peer
    )
    for k, full in enumerate((allt, allo)):
        loads[6 + k].wait()
        if nz > 1:
            settle(zin.at[k, pl.ds(0, nz - 1)], az_r.at[k])
        gathered = jnp.concatenate([zin[k, i].astype(F32) for i in range(nz)], axis=0)
        full[block(core * ny + y), :] = gathered.astype(BF16)
        (t_first, o_first)[k]()

    loads[4].wait()
    loads[5].wait()
    prepared(2, wdown, pl.ds(0, height))

    t_take(t_at[0])
    t_take(t_at[1])
    o_take(o_at[0])

    split = width_of[0]
    parts = ((sum_gu, zl_gu_out, zl_gu_in, x_gu_out, x_gu_in), (sum_b, zl_b_out, zl_b_in, x_b_out, x_b_in))

    def product(k, rows_in):
        if k == 0:
            return dot(rows_in(allt), wcat[pl.ds(0, split), :], (1, 1))
        back = dot(rows_in(allo), wdown[...], (1, 1))
        tail = dot(rows_in(allt), wcat[pl.ds(split, 2 * height - split), :], (1, 1))
        return jnp.concatenate([back, tail], axis=1)

    def early(k, offsets):
        out, arriving = parts[k][1:3]
        spots = [lax.rem(y + by, ny) for by in offsets]
        formed = product(
            k, lambda full: jnp.concatenate([full[block((1 - zl) * ny + at), :] for at in spots], axis=0)
        ).astype(BF16)
        for i, at in enumerate(spots):
            out[block(at), :] = formed[i * TILE : (i + 1) * TILE, :]
            send(out.at[block(at), :], arriving.at[block(at), :], sent.at[4 + k], bz_r.at[k, at], zl_peer)

    def pair(k, at):
        total, _, arrived, out, _ = parts[k]
        there = block(at)
        settle(arrived.at[there, :], bz_r.at[k, at])
        out[there, :] = (total[there, :] + arrived[there, :].astype(F32)).astype(BF16)

    def pass_on(k, at, by):
        out, into = parts[k][3:]
        send(out.at[block(at), :], into.at[by], sent.at[6 + k], bx_r.at[k], (at * nl + zl, col))

    near = [0] + routes(ny)[0]
    distant = [by for by in range(1, ny) if by not in near]
    t_rest_near()
    early(0, near)
    t_take(t_at[2])
    t_rest_far()
    if distant:
        early(0, distant)
    sum_gu[...] = product(0, lambda full: full[part(zl), :])

    def pairs(k, offsets):
        for by in offsets:
            at = lax.rem(y + by, ny)
            pair(k, at)

            @pl.when(at != x)
            def _():
                pass_on(k, at, lax.rem(at + nx - x, nx))

    pairs(0, near)
    o_take(o_at[1])
    o_rest_near()
    early(1, near)
    o_take(o_at[2])
    o_rest_far()
    if distant:
        early(1, distant)
    sum_b[...] = product(1, lambda full: full[part(zl), :])
    pairs(0, distant)
    pairs(1, near)
    pairs(1, distant)

    sums = []
    for k, (total, _, arrived, out, into) in enumerate(parts):
        here = block(x)
        value = total[here, :] + arrived[here, :].astype(F32)
        settle(into.at[pl.ds(1, nx - 1)], bx_r.at[k])
        for by in range(1, nx):
            value = value + into[by].astype(F32)
        sums.append(value)

    gate, back = sums[0][:, :height], sums[1][:, :height]
    up = jnp.concatenate([sums[0][:, height:], sums[1][:, height:]], axis=1)
    logistic = 1.0 / (1.0 + jnp.exp(-gate))
    swish = gate * logistic
    up_grad = back * swish
    gate_grad = back * up * logistic * (1.0 + gate * (1.0 - logistic))
    mine = block(zl * nx + x)
    gu[mine, :] = jnp.concatenate([gate_grad, up_grad], axis=1).astype(BF16)
    g_first, g_take, (g_rest, _, _), g_drained, g_at = spread(
        gu, zl * nx, x, nx, x_peer, sent.at[8], cx_r.at[0], cz_r.at[0], zl_peer, straight=True
    )
    h_first, h_take, (h_rest, _, _), h_drained, h_at = spread(
        hid, zl * nx, x, nx, x_peer, sent.at[9], cx_r.at[1], cz_r.at[1], zl_peer
    )
    g_first()
    hid[mine, :] = (swish * up).astype(BF16)
    g_take(g_at[0])
    h_first()
    g_take(g_at[1])
    g_take(g_at[2])
    g_rest()

    core_out[...] = dot(gu[part(1 - core), :], wcat[...], (1, 0))
    send(core_out, core_in, sent.at[10], d_r.at[0], core_peer)
    own[...] = dot(gu[part(core), :], wcat[...], (1, 0))
    settle(core_in, d_r.at[0])
    total = own[...] + core_in[...]
    own[...] = total
    y_out[...] = total.astype(BF16)
    for by in far_first(ny):
        send(y_out.at[block(lax.rem(y + by, ny)), :], y_in.at[by], sent.at[11], d_r.at[1], y_peer(by))
    h_take(h_at[0])
    h_take(h_at[1])

    gwg[...] = (dot(gu[:, :height], allt[...], (0, 0)) * keep[pl.ds(0, height), :].astype(F32)).astype(BF16)
    uwg[...] = (dot(gu[:, height:], allt[...], (0, 0)) * keep[pl.ds(height, height), :].astype(F32)).astype(BF16)

    h_take(h_at[2])
    value = own[block(y), :]
    settle(y_in.at[pl.ds(1, ny - 1)], d_r.at[1])
    for by in range(1, ny):
        value = value + y_in[by].astype(F32)
    for i in range(nz):
        z_out[i] = value[i * rows : (i + 1) * rows, :]
    for by in range(1, nz):
        send(z_out.at[lax.rem(z + by, nz)], z_in.at[by], sent.at[12], d_r.at[2], z_peer(by))

    h_rest()
    dwg[...] = (dot(hid[...], allo[...], (0, 0)) * keep[pl.ds(2 * height, height), :].astype(F32)).astype(BF16)
    for k in range(2):
        if nz > 1:
            settle(zin.at[k, pl.ds(0, nz - 1)], sent.at[k])
    for drained in (t_drained, o_drained, g_drained, h_drained):
        drained()
    settle(zl_gu_out, sent.at[4])
    settle(zl_b_out, sent.at[5])
    settle(x_gu_out.at[pl.ds(0, (nx - 1) * TILE), :], sent.at[6])
    settle(x_b_out.at[pl.ds(0, (nx - 1) * TILE), :], sent.at[7])
    settle(core_out, sent.at[10])
    settle(y_out.at[pl.ds(0, (ny - 1) * TILE), :], sent.at[11])

    final = z_out[z]
    if nz > 1:
        settle(z_in.at[pl.ds(1, nz - 1)], d_r.at[2])
    for by in range(1, nz):
        final = final + z_in[by]
    ig[...] = final.astype(BF16)
    if nz > 1:
        settle(z_out.at[pl.ds(0, nz - 1)], sent.at[12])


def written(*refs):
    done = refs[-1]
    copies = [
        pltpu.make_async_copy(refs[i], refs[i + 4], done.at[i]) for i in range(4)
    ]
    for copy in copies:
        copy.start()
    for copy in copies:
        copy.wait()


def local(dims, tokens, out_grad, gate_weight, up_weight, down_weight, gate_mask, up_mask, down_mask):
    nx, nl, ny, nz, nc = dims
    rows, width = tokens.shape
    height = down_weight.shape[0]
    half = ny * TILE
    lead = 2 * height // 128 * 128
    lag = 3 * height - lead
    dma = pltpu.SemaphoreType.DMA
    vmem = pl.BlockSpec(memory_space=pltpu.VMEM)
    weight = jax.ShapeDtypeStruct((height, width), BF16)
    scratch = [
        pltpu.VMEM((2, nz, rows, width), BF16),
        pltpu.VMEM((2 * half, width), BF16),
        pltpu.VMEM((2 * half, width), BF16),
        pltpu.VMEM((2 * height, width), BF16),
        pltpu.VMEM((height, width), BF16),
        pltpu.VMEM((3 * height, width), BF16),
        pltpu.VMEM((3, width // 4, height // 4), jnp.int32),
        pltpu.VMEM((half, lead), BF16),
        pltpu.VMEM((half, lead), BF16),
        pltpu.VMEM((half, lag), BF16),
        pltpu.VMEM((half, lag), BF16),
        pltpu.VMEM((half, lead), F32),
        pltpu.VMEM((half, lag), F32),
        pltpu.VMEM((half, lead), BF16),
        pltpu.VMEM((nx, TILE, lead), BF16),
        pltpu.VMEM((half, lag), BF16),
        pltpu.VMEM((nx, TILE, lag), BF16),
        pltpu.VMEM((2 * half, 2 * height), BF16),
        pltpu.VMEM((2 * half, height), BF16),
        pltpu.VMEM((half, width), F32),
        pltpu.VMEM((half, width), F32),
        pltpu.VMEM((half, width), F32),
        pltpu.VMEM((half, width), BF16),
        pltpu.VMEM((ny, TILE, width), BF16),
        pltpu.VMEM((nz, rows, width), F32),
        pltpu.VMEM((nz, rows, width), F32),
        dma((8,)), dma((13,)), dma((2,)), dma((2, ny)), dma((2, 2)),
        dma((2, nx)), dma((2,)), dma((2, nx)), dma((2, 2)), dma((3,)),
    ]
    held = (jax.ShapeDtypeStruct((rows, width), BF16), weight, weight, weight)
    results = pl.pallas_call(
        functools.partial(kernel, dims),
        out_shape=held,
        in_specs=[pl.BlockSpec(memory_space=pltpu.HBM)] * 8,
        out_specs=(vmem,) * 4,
        scratch_shapes=scratch,
        compiler_params=pltpu.CompilerParams(
            collective_id=0, has_side_effects=True, vmem_limit_bytes=40 * 1024 * 1024
        ),
        name="block",
    )(
        *(
            pltpu.with_memory_space_constraint(a, pltpu.HBM)
            for a in (
                tokens, out_grad, gate_weight.T, up_weight.T, down_weight,
                gate_mask, up_mask, down_mask.T,
            )
        )
    )
    input_grad, gate_wg, up_wg, down_wg = pl.pallas_call(
        written,
        out_shape=held,
        in_specs=[pl.BlockSpec(memory_space=pl.ANY)] * 4,
        out_specs=(pl.BlockSpec(memory_space=pl.ANY),) * 4,
        scratch_shapes=[dma((4,))],
        compiler_params=pltpu.CompilerParams(vmem_limit_bytes=2 * 1024 * 1024),
        name="write",
    )(*results)
    return input_grad, gate_wg.T, up_wg.T, down_wg


def solution(mesh, dims=(8, 2, 8, 4, 2)):
    in_specs = (
        P("col", "row"),
        P("col", "row"),
        P("row", "col"),
        P("row", "col"),
        P("col", "row"),
        P("row", "col"),
        P("row", "col"),
        P("col", "row"),
    )
    out_specs = (P("col", "row"), P("row", "col"), P("row", "col"), P("col", "row"))
    return jax.shard_map(
        functools.partial(local, dims), mesh=mesh, in_specs=in_specs, out_specs=out_specs, check_vma=False
    )
```
